256 devices in a mesh: ens: 4 (over y), horiz: 64 (over x, z, core).
Axes of the slice: x: 4, y: 4, z: 8, core: 2. Of those that a mesh axis runs over, the one named last changes fastest.
Arguments:
- prognostic: float32 [4, 128, 256, 128], P('ens', None, 'horiz'), may hold values from -6 to 6
- diffusivity: float32 [4, 32, 256, 128], P('ens', None, 'horiz'), may hold values from 0.1 to 10
- mixing: float32 [2, 256, 128], P(None, 'horiz'), may hold values from 0.03 to 0.24
- cotangent: float32 [4, 128, 256, 128], P('ens', None, 'horiz'), may hold values from -6 to 6
- tile_cols: int32 [4, 64, 3, 128], P('ens', 'horiz'), may hold values from 0 to 511, as said below
- pad_mask: int32 [4, 64, 3, 128], P('ens', 'horiz'), may hold values 0 or 1
- tile_count: int32 [4, 64], P('ens', 'horiz'), may hold values from 1 to 3, as said below
- w_in: bfloat16 [1024, 128], replicated, may hold values from -0.5 to 0.5
- w_mid: bfloat16 [1024, 1024], replicated, may hold values from -0.1875 to 0.1875
- w_out: bfloat16 [128, 1024], replicated, may hold values from -0.1875 to 0.1875
Outputs:
- state_next: float32 [4, 128, 256, 128], P('ens', None, 'horiz')
- state_grad: float32 [4, 128, 256, 128], P('ens', None, 'horiz')
- grad_in: float32 [1024, 128], replicated
- grad_mid: float32 [1024, 1024], replicated
- grad_out: float32 [128, 1024], replicated
The draws below stay inside these ranges and needn't reach their ends.
Inputs may be any that keep to these rules, and one draw needn't show every extreme that they name: `tile_cols`: within one member and block all 3 x 128 entries name different columns. Tiles 0 to tile_count - 1 of a block are in use; in every member some block uses all 3.
All inputs are finite; a program needn't handle non-finite values. No bound on the sum of `pad_mask` on one device may be relied on, other than what follows from the above.
Results may differ from the reference program's by a relative error of at most 0.0071.
Values may be sent and summed in bfloat16 or wider, within the bound.
A program may use at most 64 MiB of HBM per device.

```python
import math
import jax
import jax.numpy as jnp
from jax import lax

LEVELS = 32
UNITS = 1024
LATITUDES = 128
TILE_COLS = 128
DYN_STEPS = 2
FIELDS = 128
CELLS = 512
TILES_DEV = 3
MEMBERS = 4
BLOCKS = 64
LONGITUDES = 256
COLUMNS = 131072


def draw_tile_cols(key, part):
    block_keys = jax.random.split(key, MEMBERS * BLOCKS)

    def one_block(block_key):
        return jax.random.permutation(block_key, CELLS)[:TILES_DEV * TILE_COLS]
    picked = jax.vmap(one_block)(block_keys)
    return picked.reshape(MEMBERS, BLOCKS, TILES_DEV, TILE_COLS).astype(jnp.int32)


def draw_tile_count(key, part):
    draw_key, pick_key = jax.random.split(key)
    spread_draw = jax.random.randint(draw_key, (MEMBERS, BLOCKS), 0, TILES_DEV)
    counts = 1 + spread_draw * spread_draw // TILES_DEV
    busiest = jax.random.randint(pick_key, (MEMBERS, 1), 0, BLOCKS)
    block_index = jnp.arange(BLOCKS)[None, :]
    return jnp.where(block_index == busiest, TILES_DEV, counts).astype(jnp.int32)


def set_ends(entries, own_key, least, largest):
    place = [jax.random.randint(jax.random.fold_in(own_key, axis), (), 0, length) for axis, length in enumerate(entries.shape)]
    longest = entries.shape.index(max(entries.shape))
    next_to = place[:longest] + [(place[longest] + 1) % entries.shape[longest]] + place[longest + 1:]
    return entries.at[tuple(place)].set(least).at[tuple(next_to)].set(largest)


def steps_of(stream_key, dims, shards, least, high):
    gain, own = 1.0, jax.random.fold_in(stream_key, 6)
    for axis_at, parts in shards:
        draws = jnp.exp(jax.random.uniform(jax.random.fold_in(own, axis_at), (parts,), jnp.float32, least / len(shards), high / len(shards)))
        gain = gain * jnp.repeat(draws, dims[axis_at] // parts).reshape([-1 if axis == axis_at else 1 for axis in range(len(dims))])
    return gain


def bell_draw(rng, extent, deviation, most, pieces=(), held_as=jnp.bfloat16):
    values = jax.random.normal(rng, extent, jnp.float32) * deviation
    if len(pieces) > 0:
        values = steps_of(rng, extent, pieces, -0.22, 0.18) * values
    return jnp.clip(values, min=-most, max=most).astype(held_as)


def setup_inputs(seed: int = 0) -> dict:
    key_of = jax.random.split(jax.random.key(seed), 11)
    prognostic = bell_draw(key_of[0], (MEMBERS, FIELDS, LONGITUDES, LATITUDES), 1.0, 6.0, ((0, 4), (2, 64)), jnp.float32)
    diffusivity = jnp.clip(jnp.exp(math.log(10.0) - 4.6051702 * jax.random.uniform(key_of[1], (MEMBERS, LEVELS, LONGITUDES, LATITUDES), jnp.float32) ** steps_of(key_of[1], (MEMBERS, LEVELS, LONGITUDES, LATITUDES), ((0, 4), (2, 64)), -0.2, 0.2)), 0.1, 10.0)
    mixing = jnp.clip(jnp.exp(math.log(0.24) - 2.0794415 * jax.random.uniform(key_of[2], (2, LONGITUDES, LATITUDES), jnp.float32) ** steps_of(key_of[2], (2, LONGITUDES, LATITUDES), ((1, 64),), -0.2, 0.2)), 0.03, 0.24)
    cotangent = bell_draw(key_of[3], (MEMBERS, FIELDS, LONGITUDES, LATITUDES), 1.0, 6.0, ((0, 4), (2, 64)), jnp.float32)
    tile_cols = draw_tile_cols(jax.random.fold_in(key_of[10], 71), 0)
    pad_mask = set_ends((jax.random.randint(key_of[5], (MEMBERS, BLOCKS, TILES_DEV, TILE_COLS), 0, 4) < 3).astype(jnp.int32), jax.random.fold_in(key_of[5], 1), 0, 1)
    tile_count = draw_tile_count(jax.random.fold_in(key_of[10], 71), 0)
    w_in = bell_draw(key_of[7], (UNITS, FIELDS), FIELDS ** -0.5, 0.5)
    w_mid = bell_draw(key_of[8], (UNITS, UNITS), UNITS ** -0.5, 0.1875)
    w_out = bell_draw(key_of[9], (FIELDS, UNITS), UNITS ** -0.5, 0.1875)
    return dict(prognostic=prognostic, diffusivity=diffusivity, mixing=mixing, cotangent=cotangent, tile_cols=tile_cols, pad_mask=pad_mask, tile_count=tile_count, w_in=w_in, w_mid=w_mid, w_out=w_out)


def stencil_step(field_now, coef_lon, coef_lat):
    east_flux = coef_lon * (jnp.roll(field_now, -1, axis=-2) - field_now)
    west_flux = jnp.roll(east_flux, 1, axis=-2)
    rising = jnp.concatenate([field_now[..., 1:] - field_now[..., :-1], jnp.zeros_like(field_now[..., :1])], axis=-1)
    north_flux = coef_lat * rising
    south_flux = jnp.concatenate([jnp.zeros_like(north_flux[..., :1]), north_flux[..., :-1]], axis=-1)
    return field_now + east_flux - west_flux + (north_flux - south_flux)

def evolve(field_now, mixing):
    for repeat in range(DYN_STEPS):
        field_now = stencil_step(field_now, mixing[0], mixing[1])
    return field_now

def silu_slope(pre_act):
    sigma_val = jax.nn.sigmoid(pre_act)
    return sigma_val * (1.0 + pre_act * (1.0 - sigma_val))

def vertical_solve(coefficient, right_side):
    coef_below = jnp.concatenate([jnp.zeros_like(coefficient[:1]), coefficient[:-1]], axis=0)
    coef_above = jnp.concatenate([coefficient[:-1], jnp.zeros_like(coefficient[:1])], axis=0)
    diag_term = 1.0 + coef_below + coefficient
    by_level = jnp.transpose(right_side, (1, 0, 2))

    def sweep_down(carried, inputs):
        prev_ratio, prev_value = carried
        below_now, above_now, diag_now, right_now = inputs
        divisor = diag_now + below_now * prev_ratio
        ratio_now = -above_now / divisor
        value_now = (right_now + below_now * prev_value) / divisor
        return ((ratio_now, value_now), (ratio_now, value_now))
    start_state = (jnp.zeros_like(coefficient[0]), jnp.zeros_like(by_level[0]))
    _, (ratios, values) = lax.scan(sweep_down, start_state, (coef_below, coef_above, diag_term, by_level))

    def sweep_up(carried, inputs):
        ratio_now, value_now = inputs
        result = value_now - ratio_now * carried
        return (result, result)
    _, solved = lax.scan(sweep_up, jnp.zeros_like(by_level[0]), (ratios, values), reverse=True)
    return jnp.transpose(solved, (1, 0, 2))

def column_physics(x_tile, coef_tile, cot_tile, w_in, w_mid, w_out):
    fields = x_tile.shape[0]
    levels = coef_tile.shape[0]
    var_count = fields // levels
    contract_cols = (((1,), (1,)), ((), ()))
    contract_rows = (((0,), (0,)), ((), ()))
    pre_one = jnp.dot(w_in, x_tile, preferred_element_type=jnp.float32)
    act_one = jax.nn.silu(pre_one).astype(jnp.bfloat16)
    pre_two = jnp.dot(w_mid, act_one, preferred_element_type=jnp.float32)
    act_two = jax.nn.silu(pre_two).astype(jnp.bfloat16)
    tendency = jnp.dot(w_out, act_two, preferred_element_type=jnp.float32)
    coefficient = coef_tile.astype(jnp.float32)
    forced = (x_tile.astype(jnp.float32) + tendency).reshape(var_count, levels, -1)
    new_tile = vertical_solve(coefficient, forced).reshape(fields, -1)
    adjoint = vertical_solve(coefficient, cot_tile.astype(jnp.float32).reshape(var_count, levels, -1)).reshape(fields, -1)
    adjoint_half = adjoint.astype(jnp.bfloat16)
    grad_out = lax.dot_general(adjoint_half, act_two, contract_cols, preferred_element_type=jnp.float32)
    back_two = lax.dot_general(w_out, adjoint_half, contract_rows, preferred_element_type=jnp.float32)
    delta_two = (back_two * silu_slope(pre_two)).astype(jnp.bfloat16)
    grad_mid = lax.dot_general(delta_two, act_one, contract_cols, preferred_element_type=jnp.float32)
    back_one = lax.dot_general(w_mid, delta_two, contract_rows, preferred_element_type=jnp.float32)
    delta_one = (back_one * silu_slope(pre_one)).astype(jnp.bfloat16)
    grad_in = lax.dot_general(delta_one, x_tile, contract_cols, preferred_element_type=jnp.float32)
    grad_x = adjoint + lax.dot_general(w_in, delta_one, contract_rows, preferred_element_type=jnp.float32)
    return (new_tile.astype(jnp.bfloat16), grad_x.astype(jnp.bfloat16), grad_in, grad_mid, grad_out)

def to_blocks(field_now):
    members, row_count, longitudes, latitudes = field_now.shape
    split_view = field_now.reshape(members, row_count, BLOCKS, longitudes // BLOCKS * latitudes)
    return jnp.transpose(split_view, (0, 2, 1, 3))

def from_blocks(blocks, full_shape):
    return jnp.transpose(blocks, (0, 2, 1, 3)).reshape(full_shape)

def gather_tiles(blocks, tile_cols):

    def one_block(block_vals, columns):
        return block_vals[:, columns.reshape(-1)]
    picked = jax.vmap(jax.vmap(one_block))(blocks, tile_cols)
    members, block_total, row_count, _ = picked.shape
    return jnp.transpose(picked.reshape(members, block_total, row_count, TILES_DEV, TILE_COLS), (0, 1, 3, 2, 4))

def place_tiles(blocks, tile_cols, tile_vals, live_mask):

    def one_block(block_vals, columns, vals_here, live_here):
        flat_cols = columns.reshape(-1)
        row_count = block_vals.shape[0]
        fresh_vals = jnp.transpose(vals_here, (1, 0, 2)).reshape(row_count, -1).astype(jnp.float32)
        kept_vals = block_vals[:, flat_cols]
        return block_vals.at[:, flat_cols].set(jnp.where(live_here.reshape(-1)[None, :] > 0, fresh_vals, kept_vals))
    return jax.vmap(jax.vmap(one_block))(blocks, tile_cols, tile_vals, live_mask)

def flatten_tiles(tiles_arr):
    return tiles_arr.reshape((-1,) + tiles_arr.shape[3:])

def reference(prognostic, diffusivity, mixing, cotangent, tile_cols, pad_mask, tile_count, w_in, w_mid, w_out):
    moved = evolve(prognostic, mixing)
    tile_index = jnp.arange(TILES_DEV, dtype=jnp.int32)
    active = tile_index[None, None, :] < tile_count[:, :, None]
    live_mask = pad_mask * active[..., None].astype(jnp.int32)
    x_tiles = gather_tiles(to_blocks(moved), tile_cols).astype(jnp.bfloat16)
    coef_tiles = gather_tiles(to_blocks(diffusivity), tile_cols).astype(jnp.bfloat16)
    cot_tiles = (gather_tiles(to_blocks(cotangent), tile_cols) * live_mask[:, :, :, None, :].astype(jnp.float32)).astype(jnp.bfloat16)

    def visit(carried, inputs):
        sum_in, sum_mid, sum_out = carried
        x_tile, coef_tile, cot_tile, live_flag = inputs

        def compute(operands):
            return column_physics(operands[0], operands[1], operands[2], w_in, w_mid, w_out)

        def skip_tile(operands):
            return (jnp.zeros((FIELDS, TILE_COLS), jnp.bfloat16), jnp.zeros((FIELDS, TILE_COLS), jnp.bfloat16), jnp.zeros((UNITS, FIELDS), jnp.float32), jnp.zeros((UNITS, UNITS), jnp.float32), jnp.zeros((FIELDS, UNITS), jnp.float32))
        results = lax.cond(live_flag, compute, skip_tile, (x_tile, coef_tile, cot_tile))
        return ((sum_in + results[2], sum_mid + results[3], sum_out + results[4]), (results[0], results[1]))
    start_sums = (jnp.zeros((UNITS, FIELDS), jnp.float32), jnp.zeros((UNITS, UNITS), jnp.float32), jnp.zeros((FIELDS, UNITS), jnp.float32))
    sums, (new_tiles, grad_tiles) = lax.scan(visit, start_sums, (flatten_tiles(x_tiles), flatten_tiles(coef_tiles), flatten_tiles(cot_tiles), active.reshape(-1)))
    new_tiles = new_tiles.reshape(MEMBERS, BLOCKS, TILES_DEV, FIELDS, TILE_COLS)
    grad_tiles = grad_tiles.reshape(MEMBERS, BLOCKS, TILES_DEV, FIELDS, TILE_COLS)
    state_next = from_blocks(place_tiles(to_blocks(moved), tile_cols, new_tiles, live_mask), moved.shape)
    grad_field = from_blocks(place_tiles(to_blocks(cotangent), tile_cols, grad_tiles, live_mask), cotangent.shape)
    state_grad = evolve(grad_field, mixing)
    factor = 1.0 / math.sqrt(COLUMNS)
    return (state_next, state_grad, sums[0] * factor, sums[1] * factor, sums[2] * factor)
```

```python
import functools
import math

import jax
import jax.numpy as jnp
from jax import lax
from jax.experimental import pallas as pl
from jax.experimental.pallas import tpu as pltpu
from jax.sharding import PartitionSpec as P

MESH = pl.DeviceIdType.MESH
LONS = 4
CHUNKS = 5
CHUNK_ROWS = 256
F32 = jnp.float32
BF16 = jnp.bfloat16
NT = (((1,), (1,)), ((), ()))
TN = (((0,), (0,)), ((), ()))


def sigmoid(value):
    return 0.5 * jnp.tanh(0.5 * value) + 0.5


def window_kernel(
    sizes,
    factor,
    prog_hbm,
    diff_hbm,
    mix_hbm,
    cot_hbm,
    cols_hbm,
    pad_hbm,
    count_hbm,
    win_hbm,
    wmid_hbm,
    wout_hbm,
    state_ref,
    sgrad_ref,
    full_ref,
    prog,
    diff,
    mix,
    cot,
    cols,
    pad,
    count,
    w_in,
    w_mid,
    w_out,
    halo_out,
    halo_in,
    mix_in,
    mid_step,
    moved,
    recip,
    ratio,
    adj,
    forced,
    gfield,
    x_half,
    adj_half,
    back_two,
    slope_one,
    act_one,
    act_two,
    delta_one,
    delta_two,
    part_f,
    part_b,
    got0,
    sum1_f,
    sum1_b,
    got1,
    sum2_f,
    sum2_b,
    got2,
    sum3_f,
    sum3_b,
    got3,
    owned,
    zfull,
    load_sem,
    halo_send,
    halo_recv,
    s0_send,
    s0_recv,
    s1_send,
    s1_recv,
    s2_send,
    s2_recv,
    s3_send,
    s3_recv,
    g3_send,
    g3_recv,
    g2_send,
    g2_recv,
    g1_send,
    g1_recv,
    g0_send,
    g0_recv,
):
    n, nz, levels, variables = sizes
    fields = levels * variables
    units = w_mid.shape[0]
    half = units // 2
    ring = n * nz * 2
    y = lax.axis_index("ens")
    h = lax.axis_index("horiz")
    core = h % 2
    z = (h // 2) % nz
    x = h // (2 * nz)
    right = (h + 1) % ring
    left = (h + ring - 1) % ring
    partner = h + 1 - 2 * core
    pieces = 2 * n
    rows = CHUNK_ROWS // pieces
    width = half // n
    zrows = owned.shape[0]

    def at_x(step):
        return (x + step) % n

    def at_y(step):
        return (y + step) % n

    def at_z(step):
        return (z + step) % nz

    def place(xi, zi, ci):
        return (xi * nz + zi) * 2 + ci

    barrier = pltpu.get_barrier_semaphore()
    greeted = [(at_y(s), h) for s in range(1, n)]
    greeted += [(y, place(at_x(s), z, core)) for s in range(1, n)]
    greeted += [(y, place(x, at_z(s), core)) for s in range(1, nz)]
    greeted += [(y, right), (y, left)]
    for peer in greeted:
        pl.semaphore_signal(barrier, inc=1, device_id=peer, device_id_type=MESH)

    loads = []
    for slot, (source, target) in enumerate(
        [
            (prog_hbm, prog),
            (mix_hbm, mix),
            (cols_hbm, cols),
            (pad_hbm, pad),
            (count_hbm, count),
            (diff_hbm, diff),
            (cot_hbm, cot),
            (wout_hbm, w_out),
            (win_hbm, w_in),
            (wmid_hbm, w_mid),
        ]
    ):
        copy = pltpu.make_async_copy(source, target, load_sem.at[slot])
        copy.start()
        loads.append(copy)

    sent = []

    def send(src, dst, send_sem, recv_sem, peer):
        copy = pltpu.make_async_remote_copy(
            src_ref=src,
            dst_ref=dst,
            send_sem=send_sem,
            recv_sem=recv_sem,
            device_id=peer,
            device_id_type=MESH,
        )
        copy.start()
        sent.append(copy)
        return copy

    def lon_rows(lon):
        return pl.ds(lon, fields, stride=LONS)

    def lon_cols(lon):
        return pl.ds(lon * 128, 128)

    def send_halo(which):
        return [
            send(
                halo_out.at[which, 0],
                halo_in.at[which, 0],
                halo_send.at[which, 0],
                halo_recv.at[which, 0],
                (y, right),
            ),
            send(
                halo_out.at[which, 1],
                halo_in.at[which, 1],
                halo_send.at[which, 1],
                halo_recv.at[which, 1],
                (y, left),
            ),
        ]

    loads[0].wait()
    for lon in range(LONS):
        halo_out[0, 1 - lon // 2, lon % 2] = prog[lon_rows(lon), :].astype(BF16)
    loads[1].wait()
    pl.semaphore_wait(barrier, len(greeted))
    halo_one = send_halo(0)
    mix_copies = [
        send(mix, mix_in.at[0], halo_send.at[2, 0], halo_recv.at[2, 0], (y, right)),
        send(mix, mix_in.at[1], halo_send.at[2, 1], halo_recv.at[2, 1], (y, left)),
    ]

    for copy in loads[2:7]:
        copy.wait()
    lon_of = lax.broadcasted_iota(jnp.int32, (16, 128), 0)
    lat_of = lax.broadcasted_iota(jnp.int32, (128, 128), 0)
    used = count[0, 0]
    live = jnp.zeros((16, 128), F32)
    for tile in range(cols.shape[0]):
        column = cols[tile]
        flag = jnp.where(tile < used, pad[tile], 0)
        lon_hit = (lon_of == column // 128) & (jnp.broadcast_to(flag, (16, 128)) > 0)
        lat_hit = lat_of == column % 128
        live = live + lax.dot_general(
            jnp.where(lon_hit, 1.0, 0.0).astype(BF16),
            jnp.where(lat_hit, 1.0, 0.0).astype(BF16),
            NT,
            preferred_element_type=F32,
        )
    live4 = live[:LONS]

    def level_rows(var, level):
        return pl.ds((var * levels + level) * LONS, LONS)

    def coefficient(level):
        return diff[level * LONS : (level + 1) * LONS, :].astype(BF16).astype(F32)

    below = jnp.zeros((LONS, 128), F32)
    last_ratio = jnp.zeros((LONS, 128), F32)
    for level in range(levels):
        here = coefficient(level)
        inverse = 1.0 / (1.0 + below + here + below * last_ratio)
        last_ratio = -here * inverse
        recip[level * LONS : (level + 1) * LONS, :] = inverse
        ratio[level * LONS : (level + 1) * LONS, :] = last_ratio
        below = here

    def solve(load_right, work, store):
        value = [jnp.zeros((LONS, 128), F32) for _ in range(variables)]
        lower = jnp.zeros((LONS, 128), F32)
        for level in range(levels):
            inverse = recip[level * LONS : (level + 1) * LONS, :]
            for var in range(variables):
                value[var] = (load_right(var, level) + lower * value[var]) * inverse
                work[level_rows(var, level), :] = value[var]
            lower = coefficient(level)
        for var in range(variables):
            store(var, levels - 1, value[var])
        for level in range(levels - 2, -1, -1):
            back = ratio[level * LONS : (level + 1) * LONS, :]
            for var in range(variables):
                value[var] = work[level_rows(var, level), :] - back * value[var]
                store(var, level, value[var])

    def load_cot(var, level):
        return (cot[level_rows(var, level), :] * live4).astype(BF16).astype(F32)

    def store_adj(var, level, value):
        adj[level_rows(var, level), :] = value

    solve(load_cot, adj, store_adj)
    for lon in range(LONS):
        adj_half[:, lon_cols(lon)] = adj[lon_rows(lon), :].astype(BF16)
    loads[7].wait()
    back_two[...] = lax.dot_general(w_out[...], adj_half[...], TN, preferred_element_type=F32)

    for copy in mix_copies:
        copy.wait_recv()
    lane = lax.broadcasted_iota(jnp.int32, (2 * LONS, 128), 1)
    mixes = [mix_in[0], mix[...], mix_in[1]]
    norths = [jnp.where(lane == 127, 0.0, m) for m in mixes]
    souths = [jnp.where(lane == 0, 0.0, pltpu.roll(m, 1, 1)) for m in mixes]

    def mix_row(tables, lon, offset):
        row = lon % LONS + offset
        return tables[lon // LONS + 1][row : row + 1]

    weights = []
    for lon in range(-1, LONS + 1):
        east = mix_row(mixes, lon, 0)
        west = mix_row(mixes, lon - 1, 0)
        north = mix_row(norths, lon, LONS)
        south = mix_row(souths, lon, LONS)
        weights.append((1.0 - east - west - north - south, east, west, north, south))

    def stencil(lon, west_val, own, east_val):
        centre, east, west, north, south = weights[lon + 1]
        return (
            centre * own
            + east * east_val
            + west * west_val
            + north * pltpu.roll(own, 127, 1)
            + south * pltpu.roll(own, 1, 1)
        )

    def advance(which, load_own, store):
        def load(lon):
            if lon < 0:
                return halo_in[which, 0, lon + 2].astype(F32)
            if lon >= LONS:
                return halo_in[which, 1, lon - LONS].astype(F32)
            return load_own(lon)

        for lon in range(-1, LONS + 1):
            mid_step[lon + 1] = stencil(lon, load(lon - 1), load(lon), load(lon + 1))
        for lon in range(LONS):
            store(lon, stencil(lon, mid_step[lon], mid_step[lon + 1], mid_step[lon + 2]))

    def load_prog(lon):
        return prog[lon_rows(lon), :]

    def store_moved(lon, value):
        moved[lon_rows(lon), :] = value
        x_half[:, lon_cols(lon)] = value.astype(BF16)

    for copy in halo_one:
        copy.wait_recv()
    advance(0, load_prog, store_moved)

    loads[8].wait()
    for block in range(units // CHUNK_ROWS):
        span = slice(block * CHUNK_ROWS, (block + 1) * CHUNK_ROWS)
        pre = jnp.dot(w_in[span, :], x_half[...], preferred_element_type=F32)
        sig = sigmoid(pre)
        act_one[span, :] = (pre * sig).astype(BF16)
        slope_one[span, :] = sig * (1.0 + pre * (1.0 - sig))

    def keep_chunk(chunk, first_row, value):
        for piece in range(value.shape[0] // rows):
            strip = value[piece * rows : (piece + 1) * rows, :]
            slot = first_row // rows + piece
            for side in range(2):
                block = strip[:, side * half : (side + 1) * half]
                part_f[side, chunk, slot] = block
                part_b[side, chunk, slot] = block.astype(BF16)

    s0 = []

    def send_s0(chunk):
        s0.append(
            send(
                part_b.at[1 - core, chunk],
                got0.at[chunk],
                s0_send.at[chunk],
                s0_recv.at[chunk],
                (y, partner),
            )
        )

    s1 = []

    def send_s1(chunk):
        s0[chunk].wait_recv()
        total = part_f[core, chunk] + got0[chunk].astype(F32)
        sum1_f[chunk] = total
        sum1_b[chunk] = total.astype(BF16)
        copies = ([], [])
        for step in range(1, n):
            copies[0].append(
                send(
                    sum1_b.at[chunk, at_x(step)],
                    got1.at[0, chunk, step - 1],
                    s1_send.at[0, chunk, step - 1],
                    s1_recv.at[0, chunk, step - 1],
                    (y, place(at_x(step), z, core)),
                )
            )
            copies[1].append(
                send(
                    sum1_b.at[chunk, n + at_y(step)],
                    got1.at[1, chunk, step - 1],
                    s1_send.at[1, chunk, step - 1],
                    s1_recv.at[1, chunk, step - 1],
                    (at_y(step), h),
                )
            )
        s1.append(copies)

    loads[9].wait()
    for block in range(units // CHUNK_ROWS):
        span = slice(block * CHUNK_ROWS, (block + 1) * CHUNK_ROWS)
        pre = jnp.dot(w_mid[span, :], act_one[...], preferred_element_type=F32)
        sig = sigmoid(pre)
        act_two[span, :] = (pre * sig).astype(BF16)
        delta = (back_two[span, :] * (sig * (1.0 + pre * (1.0 - sig)))).astype(BF16)
        delta_two[span, :] = delta
        keep_chunk(
            block, 0, lax.dot_general(delta, act_one[...], NT, preferred_element_type=F32)
        )
        send_s0(block)
        if block >= 1:
            send_s1(block - 1)

    keep_chunk(
        CHUNKS - 1,
        0,
        lax.dot_general(adj_half[...], act_two[...], NT, preferred_element_type=F32),
    )
    for block in range(units // CHUNK_ROWS):
        span = slice(block * CHUNK_ROWS, (block + 1) * CHUNK_ROWS)
        back = lax.dot_general(w_mid[:, span], delta_two[...], TN, preferred_element_type=F32)
        delta_one[span, :] = (back * slope_one[span, :]).astype(BF16)
    send_s1(CHUNKS - 2)
    grad_in = lax.dot_general(delta_one[...], x_half[...], NT, preferred_element_type=F32)
    keep_chunk(
        CHUNKS - 1,
        CHUNK_ROWS // 2,
        jnp.concatenate(
            [grad_in[b * 128 : (b + 1) * 128, :] for b in range(units // 128)], axis=1
        ),
    )
    send_s0(CHUNKS - 1)

    back_x = lax.dot_general(w_in[...], delta_one[...], TN, preferred_element_type=F32)
    for lon in range(LONS):
        fresh = adj[lon_rows(lon), :] + back_x[:, lon * 128 : (lon + 1) * 128]
        value = jnp.where(
            jnp.broadcast_to(live[lon : lon + 1], (fields, 128)) > 0.5,
            fresh.astype(BF16).astype(F32),
            cot[lon_rows(lon), :],
        )
        gfield[lon] = value
        halo_out[1, 1 - lon // 2, lon % 2] = value.astype(BF16)
    halo_two = send_halo(1)
    send_s1(CHUNKS - 1)

    tendency = jnp.dot(w_out[...], act_two[...], preferred_element_type=F32)
    for lon in range(LONS):
        forced[lon_rows(lon), :] = (
            x_half[:, lon_cols(lon)].astype(F32) + tendency[:, lon * 128 : (lon + 1) * 128]
        )

    def load_forced(var, level):
        return forced[level_rows(var, level), :]

    def store_state(var, level, value):
        here = level_rows(var, level)
        state_ref[here, :] = jnp.where(
            live4 > 0.5, value.astype(BF16).astype(F32), moved[here, :]
        )

    solve(load_forced, forced, store_state)

    own1 = (x, n + y)
    own2 = (y, x)
    s2 = []
    for chunk in range(CHUNKS):
        copies = ([], [])
        for colour in range(2):
            total = sum1_f[chunk, own1[colour]]
            for step in range(n - 1):
                s1[chunk][colour][step].wait_recv()
                total = total + got1[colour, chunk, step].astype(F32)
            for slot in range(n):
                block = total[:, slot * width : (slot + 1) * width]
                sum2_f[colour, chunk, slot] = block
                sum2_b[colour, chunk, slot] = block.astype(BF16)
            for step in range(1, n):
                target = at_y(step) if colour == 0 else at_x(step)
                peer = (target, h) if colour == 0 else (y, place(target, z, core))
                copies[colour].append(
                    send(
                        sum2_b.at[colour, chunk, target],
                        got2.at[colour, chunk, step - 1],
                        s2_send.at[colour, chunk, step - 1],
                        s2_recv.at[colour, chunk, step - 1],
                        peer,
                    )
                )
        s2.append(copies)

    def load_gfield(lon):
        return gfield[lon]

    def store_sgrad(lon, value):
        sgrad_ref[lon_rows(lon), :] = value

    for copy in halo_two:
        copy.wait_recv()
    advance(1, load_gfield, store_sgrad)

    strip = CHUNKS * rows
    if zrows * nz > 2 * strip:
        sum3_f[2 * strip :, :] = jnp.zeros((zrows * nz - 2 * strip, width), F32)
        sum3_b[2 * strip :, :] = jnp.zeros((zrows * nz - 2 * strip, width), BF16)
    for colour in range(2):
        for chunk in range(CHUNKS):
            total = sum2_f[colour, chunk, own2[colour]]
            for step in range(n - 1):
                s2[chunk][colour][step].wait_recv()
                total = total + got2[colour, chunk, step].astype(F32)
            first = colour * strip + chunk * rows
            sum3_f[first : first + rows, :] = total
            sum3_b[first : first + rows, :] = total.astype(BF16)

    def z_rows(zi):
        return pl.ds(pl.multiple_of(zi * zrows, 16), zrows)

    s3 = [
        send(
            sum3_b.at[z_rows(at_z(step)), :],
            got3.at[step - 1],
            s3_send.at[step - 1],
            s3_recv.at[step - 1],
            (y, place(x, at_z(step), core)),
        )
        for step in range(1, nz)
    ]
    total = sum3_f[z_rows(z), :]
    for step in range(nz - 1):
        s3[step].wait_recv()
        total = total + got3[step].astype(F32)
    owned[...] = (total * factor).astype(BF16)
    zfull[z_rows(z), :] = owned[...]
    g3 = [
        send(
            owned,
            zfull.at[z_rows(z), :],
            g3_send.at[step - 1],
            g3_recv.at[step - 1],
            (y, place(x, at_z(step), core)),
        )
        for step in range(1, nz)
    ]
    for copy in g3:
        copy.wait_recv()

    g2 = ([], [])
    for colour in range(2):
        band = pl.ds(colour * strip, strip)
        slot = (x, y) if colour == 0 else (y, x)
        full_ref[core, colour, slot[0], slot[1]] = zfull[band, :]
        for step in range(1, n):
            peer = (at_y(step), h) if colour == 0 else (y, place(at_x(step), z, core))
            g2[colour].append(
                send(
                    zfull.at[band, :],
                    full_ref.at[core, colour, slot[0], slot[1]],
                    g2_send.at[colour, step - 1],
                    g2_recv.at[colour, step - 1],
                    peer,
                )
            )
    g1 = ([], [])
    g0 = []

    def send_g0(colour, position, step):
        g0.append(
            send(
                full_ref.at[core, colour, position],
                full_ref.at[core, colour, position],
                g0_send.at[colour, step],
                g0_recv.at[colour, step],
                (y, partner),
            )
        )

    for colour in range(2):
        first = x if colour == 0 else y
        for copy in g2[colour]:
            copy.wait_recv()
        for step in range(1, n):
            peer = (y, place(at_x(step), z, core)) if colour == 0 else (at_y(step), h)
            g1[colour].append(
                send(
                    full_ref.at[core, colour, first],
                    full_ref.at[core, colour, first],
                    g1_send.at[colour, step - 1],
                    g1_recv.at[colour, step - 1],
                    peer,
                )
            )
        send_g0(colour, first, 0)
    for step in range(1, n):
        for colour in range(2):
            g1[colour][step - 1].wait_recv()
            first = x if colour == 0 else y
            send_g0(colour, (first + n - step) % n, step)
    for copy in g0:
        copy.wait_recv()
    for copy in sent:
        copy.wait_send()


def unscramble_kernel(half, full_ref, mid_ref, out_ref, in_ref):
    chunk = pl.program_id(0)
    _, colours, firsts, seconds, rows, width = full_ref.shape

    def strip(colour, first):
        return [
            full_ref[side, colour, first, second].astype(F32)
            for side in range(2)
            for second in range(seconds)
        ]

    @pl.when(chunk < CHUNKS - 1)
    def _():
        for colour in range(colours):
            for first in range(firsts):
                row = (colour * firsts + first) * rows
                for slot, block in enumerate(strip(colour, first)):
                    mid_ref[row : row + rows, slot * width : (slot + 1) * width] = block

    @pl.when(chunk == CHUNKS - 1)
    def _():
        for first in range(firsts):
            row = first * rows
            for slot, block in enumerate(strip(0, first)):
                out_ref[row : row + rows, slot * width : (slot + 1) * width] = block
            for slot, block in enumerate(strip(1, first)):
                for part in range(width // 128):
                    start = (slot * (width // 128) + part) * 128 + row
                    in_ref[start : start + rows, :] = block[:, part * 128 : (part + 1) * 128]


def per_device(
    nz, prognostic, diffusivity, mixing, cotangent, tile_cols, pad_mask, tile_count, w_in, w_mid, w_out
):
    n = lax.axis_size("ens")
    fields = prognostic.shape[1]
    levels = diffusivity.shape[1]
    units = w_mid.shape[0]
    half = units // 2
    rows = CHUNK_ROWS // (2 * n)
    width = half // n
    tiles = tile_cols.shape[2]
    zrows = -(-2 * CHUNKS * rows // (16 * nz)) * 16
    flat = (fields * LONS, 128)
    factor = 1.0 / math.sqrt(n * lax.axis_size("horiz") * LONS * 128)
    dma = pltpu.SemaphoreType.DMA
    vm = pltpu.VMEM
    any_spec = pl.BlockSpec(memory_space=pl.ANY)
    vmem_spec = pl.BlockSpec(memory_space=pltpu.VMEM)
    state, sgrad, full = pl.pallas_call(
        functools.partial(window_kernel, (n, nz, levels, fields // levels), factor),
        out_shape=(
            jax.ShapeDtypeStruct(flat, F32),
            jax.ShapeDtypeStruct(flat, F32),
            jax.ShapeDtypeStruct((2, 2, n, n, CHUNKS * rows, width), BF16),
        ),
        in_specs=[any_spec] * 10,
        out_specs=(vmem_spec, vmem_spec, vmem_spec),
        scratch_shapes=[
            vm(flat, F32),
            vm((levels * LONS, 128), F32),
            vm((2 * LONS, 128), F32),
            vm(flat, F32),
            vm((tiles, 1, 128), jnp.int32),
            vm((tiles, 1, 128), jnp.int32),
            pltpu.SMEM((1, 1), jnp.int32),
            vm(w_in.shape, BF16),
            vm(w_mid.shape, BF16),
            vm(w_out.shape, BF16),
            vm((2, 2, 2, fields, 128), BF16),
            vm((2, 2, 2, fields, 128), BF16),
            vm((2, 2 * LONS, 128), F32),
            vm((LONS + 2, fields, 128), F32),
            vm(flat, F32),
            vm((levels * LONS, 128), F32),
            vm((levels * LONS, 128), F32),
            vm(flat, F32),
            vm(flat, F32),
            vm((LONS, fields, 128), F32),
            vm((fields, LONS * 128), BF16),
            vm((fields, LONS * 128), BF16),
            vm((units, LONS * 128), F32),
            vm((units, LONS * 128), F32),
            vm((units, LONS * 128), BF16),
            vm((units, LONS * 128), BF16),
            vm((units, LONS * 128), BF16),
            vm((units, LONS * 128), BF16),
            vm((2, CHUNKS, 2 * n, rows, half), F32),
            vm((2, CHUNKS, 2 * n, rows, half), BF16),
            vm((CHUNKS, 2 * n, rows, half), BF16),
            vm((CHUNKS, 2 * n, rows, half), F32),
            vm((CHUNKS, 2 * n, rows, half), BF16),
            vm((2, CHUNKS, n - 1, rows, half), BF16),
            vm((2, CHUNKS, n, rows, width), F32),
            vm((2, CHUNKS, n, rows, width), BF16),
            vm((2, CHUNKS, n - 1, rows, width), BF16),
            vm((zrows * nz, width), F32),
            vm((zrows * nz, width), BF16),
            vm((nz - 1, zrows, width), BF16),
            vm((zrows, width), BF16),
            vm((zrows * nz, width), BF16),
            dma((10,)),
            dma((3, 2)),
            dma((3, 2)),
            dma((CHUNKS,)),
            dma((CHUNKS,)),
            dma((2, CHUNKS, n - 1)),
            dma((2, CHUNKS, n - 1)),
            dma((2, CHUNKS, n - 1)),
            dma((2, CHUNKS, n - 1)),
            dma((nz - 1,)),
            dma((nz - 1,)),
            dma((nz - 1,)),
            dma((nz - 1,)),
            dma((2, n - 1)),
            dma((2, n - 1)),
            dma((2, n - 1)),
            dma((2, n - 1)),
            dma((2, n)),
            dma((2, n)),
        ],
        compiler_params=pltpu.CompilerParams(
            collective_id=0, has_side_effects=True, vmem_limit_bytes=60 * 1024 * 1024
        ),
    )(
        prognostic.reshape(flat),
        diffusivity.reshape(levels * LONS, 128),
        mixing.reshape(2 * LONS, 128),
        cotangent.reshape(flat),
        tile_cols.reshape(tiles, 1, 128),
        pad_mask.reshape(tiles, 1, 128),
        tile_count,
        w_in,
        w_mid,
        w_out,
    )
    grad_mid, grad_out, grad_in = pl.pallas_call(
        functools.partial(unscramble_kernel, half),
        grid=(CHUNKS,),
        out_shape=(
            jax.ShapeDtypeStruct(w_mid.shape, F32),
            jax.ShapeDtypeStruct(w_out.shape, F32),
            jax.ShapeDtypeStruct(w_in.shape, F32),
        ),
        in_specs=[pl.BlockSpec((2, 2, n, n, rows, width), lambda k: (0, 0, 0, 0, k, 0))],
        out_specs=(
            pl.BlockSpec((CHUNK_ROWS, units), lambda k: (jnp.minimum(k, CHUNKS - 2), 0)),
            pl.BlockSpec(w_out.shape, lambda k: (0, 0)),
            pl.BlockSpec(w_in.shape, lambda k: (0, 0)),
        ),
    )(full)
    return (
        state.reshape(prognostic.shape),
        sgrad.reshape(prognostic.shape),
        grad_in,
        grad_mid,
        grad_out,
    )


def solution(mesh):
    placed = (
        P("ens", None, "horiz", None),
        P("ens", None, "horiz", None),
        P(None, "horiz", None),
        P("ens", None, "horiz", None),
        P("ens", "horiz", None, None),
        P("ens", "horiz", None, None),
        P("ens", "horiz"),
        P(),
        P(),
        P(),
    )
    nz = mesh.shape["horiz"] // (2 * mesh.shape["ens"])
    return jax.shard_map(
        functools.partial(per_device, nz),
        mesh=mesh,
        in_specs=placed,
        out_specs=(P("ens", None, "horiz", None), P("ens", None, "horiz", None), P(), P(), P()),
        check_vma=False,
    )
```

```python
import functools
import math

import jax
import jax.numpy as jnp
from jax import lax
from jax.experimental import pallas as pl
from jax.experimental.pallas import tpu as pltpu
from jax.sharding import PartitionSpec as P

MESH = pl.DeviceIdType.MESH
LONS = 4
CHUNKS = 5
GROUPS = ((0, 1), (2, 3), (4,))
CHUNK_ROWS = 256
F32 = jnp.float32
BF16 = jnp.bfloat16
NT = (((1,), (1,)), ((), ()))
TN = (((0,), (0,)), ((), ()))


def sigmoid(value):
    return 0.5 * jnp.tanh(0.5 * value) + 0.5


def window_kernel(
    sizes,
    factor,
    prog_hbm,
    diff_hbm,
    mix_hbm,
    cot_hbm,
    cols_hbm,
    pad_hbm,
    count_hbm,
    win_hbm,
    wmid_hbm,
    wout_hbm,
    state_ref,
    sgrad_ref,
    full_ref,
    prog,
    diff,
    mix,
    cot,
    cols,
    pad,
    count,
    w_in,
    w_mid,
    w_out,
    halo_out,
    halo_in,
    mix_in,
    mid_step,
    moved,
    recip,
    ratio,
    adj,
    forced,
    gfield,
    x_half,
    adj_half,
    back_two,
    slope_one,
    act_one,
    act_two,
    delta_one,
    delta_two,
    part_f,
    part_b,
    got0,
    sum1_f,
    sum1_b,
    got1,
    sum2_f,
    sum2_b,
    got2,
    sum3_f,
    sum3_b,
    got3,
    owned,
    zfull,
    load_sem,
    halo_send,
    halo_recv,
    s0_send,
    s0_recv,
    s1_send,
    s1_recv,
    s2_send,
    s2_recv,
    s3_send,
    s3_recv,
    g3_send,
    g3_recv,
    g2_send,
    g2_recv,
    g1_send,
    g1_recv,
    g0_send,
    g0_recv,
):
    n, nz, levels, variables = sizes
    fields = levels * variables
    units = w_mid.shape[0]
    half = units // 2
    ring = n * nz * 2
    y = lax.axis_index("ens")
    h = lax.axis_index("horiz")
    core = h % 2
    z = (h // 2) % nz
    x = h // (2 * nz)
    right = (h + 1) % ring
    left = (h + ring - 1) % ring
    partner = h + 1 - 2 * core
    pieces = 2 * n
    rows = CHUNK_ROWS // pieces
    width = half // n
    zrows = owned.shape[1]

    def at_x(step):
        return (x + step) % n

    def at_y(step):
        return (y + step) % n

    def at_z(step):
        return (z + step) % nz

    def place(xi, zi, ci):
        return (xi * nz + zi) * 2 + ci

    barrier = pltpu.get_barrier_semaphore()
    greeted = [(at_y(s), h) for s in range(1, n)]
    greeted += [(y, place(at_x(s), z, core)) for s in range(1, n)]
    greeted += [(y, place(x, at_z(s), core)) for s in range(1, nz)]
    greeted += [(y, right), (y, left)]
    for peer in greeted:
        pl.semaphore_signal(barrier, inc=1, device_id=peer, device_id_type=MESH)

    loads = []
    for slot, (source, target) in enumerate(
        [
            (prog_hbm, prog),
            (mix_hbm, mix),
            (cols_hbm, cols),
            (pad_hbm, pad),
            (count_hbm, count),
            (diff_hbm, diff),
            (cot_hbm, cot),
            (wout_hbm, w_out),
            (win_hbm, w_in),
            (wmid_hbm, w_mid),
        ]
    ):
        copy = pltpu.make_async_copy(source, target, load_sem.at[slot])
        copy.start()
        loads.append(copy)

    sent = []

    def send(src, dst, send_sem, recv_sem, peer):
        copy = pltpu.make_async_remote_copy(
            src_ref=src,
            dst_ref=dst,
            send_sem=send_sem,
            recv_sem=recv_sem,
            device_id=peer,
            device_id_type=MESH,
        )
        copy.start()
        sent.append(copy)
        return copy

    def lon_rows(lon):
        return pl.ds(lon, fields, stride=LONS)

    def lon_cols(lon):
        return pl.ds(lon * 128, 128)

    def send_halo(which):
        return [
            send(
                halo_out.at[which, 0],
                halo_in.at[which, 0],
                halo_send.at[which, 0],
                halo_recv.at[which, 0],
                (y, right),
            ),
            send(
                halo_out.at[which, 1],
                halo_in.at[which, 1],
                halo_send.at[which, 1],
                halo_recv.at[which, 1],
                (y, left),
            ),
        ]

    loads[0].wait()
    for lon in range(LONS):
        halo_out[0, 1 - lon // 2, lon % 2] = prog[lon_rows(lon), :].astype(BF16)
    loads[1].wait()
    for copy in loads[2:7]:
        copy.wait()
    lon_of = lax.broadcasted_iota(jnp.int32, (16, 128), 0)
    lat_of = lax.broadcasted_iota(jnp.int32, (128, 128), 0)
    used = count[0, 0]
    live = jnp.zeros((16, 128), F32)
    for tile in range(cols.shape[0]):
        column = cols[tile]
        flag = jnp.where(tile < used, pad[tile], 0)
        lon_hit = (lon_of == column // 128) & (jnp.broadcast_to(flag, (16, 128)) > 0)
        lat_hit = lat_of == column % 128
        live = live + lax.dot_general(
            jnp.where(lon_hit, 1.0, 0.0).astype(BF16),
            jnp.where(lat_hit, 1.0, 0.0).astype(BF16),
            NT,
            preferred_element_type=F32,
        )
    live4 = live[:LONS]

    def level_rows(var, level):
        return pl.ds((var * levels + level) * LONS, LONS)

    def coefficient(level):
        return diff[level * LONS : (level + 1) * LONS, :].astype(BF16).astype(F32)

    below = jnp.zeros((LONS, 128), F32)
    last_ratio = jnp.zeros((LONS, 128), F32)
    for level in range(levels):
        here = coefficient(level)
        inverse = 1.0 / (1.0 + below + here + below * last_ratio)
        last_ratio = -here * inverse
        recip[level * LONS : (level + 1) * LONS, :] = inverse
        ratio[level * LONS : (level + 1) * LONS, :] = last_ratio
        below = here

    def sweep_down(load_right, work):
        value = [jnp.zeros((LONS, 128), F32) for _ in range(variables)]
        lower = jnp.zeros((LONS, 128), F32)
        for level in range(levels):
            inverse = recip[level * LONS : (level + 1) * LONS, :]
            for var in range(variables):
                value[var] = (load_right(var, level) + lower * value[var]) * inverse
                work[level_rows(var, level), :] = value[var]
            lower = coefficient(level)

    def sweep_up(work, store):
        value = [work[level_rows(var, levels - 1), :] for var in range(variables)]
        for var in range(variables):
            store(var, levels - 1, value[var])
        for level in range(levels - 2, -1, -1):
            back = ratio[level * LONS : (level + 1) * LONS, :]
            for var in range(variables):
                value[var] = work[level_rows(var, level), :] - back * value[var]
                store(var, level, value[var])

    def load_cot(var, level):
        return (cot[level_rows(var, level), :] * live4).astype(BF16).astype(F32)

    def store_adj(var, level, value):
        adj[level_rows(var, level), :] = value

    sweep_down(load_cot, adj)
    pl.semaphore_wait(barrier, len(greeted))
    halo_one = send_halo(0)
    mix_copies = [
        send(mix, mix_in.at[0], halo_send.at[2, 0], halo_recv.at[2, 0], (y, right)),
        send(mix, mix_in.at[1], halo_send.at[2, 1], halo_recv.at[2, 1], (y, left)),
    ]
    sweep_up(adj, store_adj)
    for lon in range(LONS):
        adj_half[:, lon_cols(lon)] = adj[lon_rows(lon), :].astype(BF16)
    loads[7].wait()
    back_two[...] = lax.dot_general(w_out[...], adj_half[...], TN, preferred_element_type=F32)

    for copy in mix_copies:
        copy.wait_recv()
    lane = lax.broadcasted_iota(jnp.int32, (2 * LONS, 128), 1)
    mixes = [mix_in[0], mix[...], mix_in[1]]
    norths = [jnp.where(lane == 127, 0.0, m) for m in mixes]
    souths = [jnp.where(lane == 0, 0.0, pltpu.roll(m, 1, 1)) for m in mixes]

    def mix_row(tables, lon, offset):
        row = lon % LONS + offset
        return tables[lon // LONS + 1][row : row + 1]

    weights = []
    for lon in range(-1, LONS + 1):
        east = mix_row(mixes, lon, 0)
        west = mix_row(mixes, lon - 1, 0)
        north = mix_row(norths, lon, LONS)
        south = mix_row(souths, lon, LONS)
        weights.append((1.0 - east - west - north - south, east, west, north, south))

    def stencil(lon, west_val, own, east_val):
        centre, east, west, north, south = weights[lon + 1]
        return (
            centre * own
            + east * east_val
            + west * west_val
            + north * pltpu.roll(own, 127, 1)
            + south * pltpu.roll(own, 1, 1)
        )

    def advance(which, load_own, store):
        def load(lon):
            if lon < 0:
                return halo_in[which, 0, lon + 2].astype(F32)
            if lon >= LONS:
                return halo_in[which, 1, lon - LONS].astype(F32)
            return load_own(lon)

        for lon in range(-1, LONS + 1):
            mid_step[lon + 1] = stencil(lon, load(lon - 1), load(lon), load(lon + 1))
        for lon in range(LONS):
            store(lon, stencil(lon, mid_step[lon], mid_step[lon + 1], mid_step[lon + 2]))

    def load_prog(lon):
        return prog[lon_rows(lon), :]

    def store_moved(lon, value):
        moved[lon_rows(lon), :] = value
        x_half[:, lon_cols(lon)] = value.astype(BF16)

    for copy in halo_one:
        copy.wait_recv()
    advance(0, load_prog, store_moved)

    loads[8].wait()
    for block in range(units // CHUNK_ROWS):
        span = slice(block * CHUNK_ROWS, (block + 1) * CHUNK_ROWS)
        pre = jnp.dot(w_in[span, :], x_half[...], preferred_element_type=F32)
        sig = sigmoid(pre)
        act_one[span, :] = (pre * sig).astype(BF16)
        slope_one[span, :] = sig * (1.0 + pre * (1.0 - sig))

    other = 1 - core

    def side_rows(side):
        return pl.ds(pl.multiple_of(side * half, half), half)

    def chunk_half(chunk, side):
        if chunk < CHUNKS - 1:
            left_side = delta_two[chunk * CHUNK_ROWS : (chunk + 1) * CHUNK_ROWS, :]
            value = lax.dot_general(
                left_side, act_one[side_rows(side), :], NT, preferred_element_type=F32
            )
        else:
            top = lax.dot_general(
                adj_half[...], act_two[side_rows(side), :], NT, preferred_element_type=F32
            )
            low = lax.dot_general(
                delta_one[side_rows(side), :], x_half[...], NT, preferred_element_type=F32
            )
            low = jnp.concatenate(
                [low[b * 128 : (b + 1) * 128, :] for b in range(half // 128)], axis=1
            )
            value = jnp.concatenate([top, low], axis=0)
        return value.reshape(pieces, rows, half)

    s0 = []

    def send_s0(chunk):
        part_b[chunk] = chunk_half(chunk, other).astype(BF16)
        s0.append(
            send(
                part_b.at[chunk],
                got0.at[chunk],
                s0_send.at[chunk],
                s0_recv.at[chunk],
                (y, partner),
            )
        )

    s1 = []

    def send_s1(chunk):
        s0[chunk].wait_recv()
        total = part_f[chunk] + got0[chunk].astype(F32)
        sum1_f[chunk] = total
        sum1_b[chunk] = total.astype(BF16)
        copies = ([], [])
        for step in range(1, n):
            copies[0].append(
                send(
                    sum1_b.at[chunk, at_x(step)],
                    got1.at[0, chunk, step - 1],
                    s1_send.at[0, chunk, step - 1],
                    s1_recv.at[0, chunk, step - 1],
                    (y, place(at_x(step), z, core)),
                )
            )
            copies[1].append(
                send(
                    sum1_b.at[chunk, n + at_y(step)],
                    got1.at[1, chunk, step - 1],
                    s1_send.at[1, chunk, step - 1],
                    s1_recv.at[1, chunk, step - 1],
                    (at_y(step), h),
                )
            )
        s1.append(copies)

    loads[9].wait()
    for block in range(units // CHUNK_ROWS):
        span = slice(block * CHUNK_ROWS, (block + 1) * CHUNK_ROWS)
        pre = jnp.dot(w_mid[span, :], act_one[...], preferred_element_type=F32)
        sig = sigmoid(pre)
        act_two[span, :] = (pre * sig).astype(BF16)
        delta = (back_two[span, :] * (sig * (1.0 + pre * (1.0 - sig)))).astype(BF16)
        delta_two[span, :] = delta

    def keep_half(chunk):
        part_f[chunk] = chunk_half(chunk, core)

    for chunk in range(CHUNKS - 1):
        send_s0(chunk)
    for chunk in range(CHUNKS - 1):
        keep_half(chunk)
        send_s1(chunk)
    for block in range(units // CHUNK_ROWS):
        span = slice(block * CHUNK_ROWS, (block + 1) * CHUNK_ROWS)
        back = lax.dot_general(w_mid[:, span], delta_two[...], TN, preferred_element_type=F32)
        delta_one[span, :] = (back * slope_one[span, :]).astype(BF16)
    send_s0(CHUNKS - 1)
    keep_half(CHUNKS - 1)
    back_x = lax.dot_general(w_in[...], delta_one[...], TN, preferred_element_type=F32)
    for lon in range(LONS):
        fresh = adj[lon_rows(lon), :] + back_x[:, lon * 128 : (lon + 1) * 128]
        value = jnp.where(
            jnp.broadcast_to(live[lon : lon + 1], (fields, 128)) > 0.5,
            fresh.astype(BF16).astype(F32),
            cot[lon_rows(lon), :],
        )
        gfield[lon] = value
        halo_out[1, 1 - lon // 2, lon % 2] = value.astype(BF16)
    halo_two = send_halo(1)
    send_s1(CHUNKS - 1)

    def tail_solve():
        tendency = jnp.dot(w_out[...], act_two[...], preferred_element_type=F32)
        for lon in range(LONS):
            forced[lon_rows(lon), :] = (
                x_half[:, lon_cols(lon)].astype(F32) + tendency[:, lon * 128 : (lon + 1) * 128]
            )

        def load_forced(var, level):
            return forced[level_rows(var, level), :]

        def store_state(var, level, value):
            here = level_rows(var, level)
            state_ref[here, :] = jnp.where(
                live4 > 0.5, value.astype(BF16).astype(F32), moved[here, :]
            )

        sweep_down(load_forced, forced)
        sweep_up(forced, store_state)

    own1 = (x, n + y)
    own2 = (y, x)
    s2, s3, g3, g2, g1, g0 = {}, {}, {}, {}, {}, {}

    def first_peer(colour, step):
        return (y, place(at_x(step), z, core)) if colour == 0 else (at_y(step), h)

    def second_peer(colour, step):
        return (at_y(step), h) if colour == 0 else (y, place(at_x(step), z, core))

    def send_s2(group):
        for chunk in GROUPS[group]:
            for colour in range(2):
                total = sum1_f[chunk, own1[colour]]
                for step in range(n - 1):
                    s1[chunk][colour][step].wait_recv()
                    total = total + got1[colour, chunk, step].astype(F32)
                for slot in range(n):
                    block = total[:, slot * width : (slot + 1) * width]
                    sum2_f[colour, chunk, slot] = block
                    sum2_b[colour, chunk, slot] = block.astype(BF16)
                for step in range(1, n):
                    s2[chunk, colour, step] = send(
                        sum2_b.at[colour, chunk, at_y(step) if colour == 0 else at_x(step)],
                        got2.at[colour, chunk, step - 1],
                        s2_send.at[colour, chunk, step - 1],
                        s2_recv.at[colour, chunk, step - 1],
                        second_peer(colour, step),
                    )

    def z_rows(zi):
        return pl.ds(pl.multiple_of(zi * zrows, 16), zrows)

    def z_peer(step):
        return (y, place(x, at_z(step), core))

    def send_s3(group):
        chunks = GROUPS[group]
        filled = 2 * len(chunks) * rows
        if zrows * nz > filled:
            sum3_f[group, filled:, :] = jnp.zeros((zrows * nz - filled, width), F32)
            sum3_b[group, filled:, :] = jnp.zeros((zrows * nz - filled, width), BF16)
        for colour in range(2):
            for slot, chunk in enumerate(chunks):
                total = sum2_f[colour, chunk, own2[colour]]
                for step in range(1, n):
                    s2[chunk, colour, step].wait_recv()
                    total = total + got2[colour, chunk, step - 1].astype(F32)
                start = (colour * len(chunks) + slot) * rows
                sum3_f[group, start : start + rows, :] = total
                sum3_b[group, start : start + rows, :] = total.astype(BF16)
        for step in range(1, nz):
            s3[group, step] = send(
                sum3_b.at[group, z_rows(at_z(step)), :],
                got3.at[group, step - 1],
                s3_send.at[group, step - 1],
                s3_recv.at[group, step - 1],
                z_peer(step),
            )

    def send_g3(group):
        total = sum3_f[group, z_rows(z), :]
        for step in range(1, nz):
            s3[group, step].wait_recv()
            total = total + got3[group, step - 1].astype(F32)
        mine = (total * factor).astype(BF16)
        owned[group] = mine
        zfull[group, z_rows(z), :] = mine
        for step in range(1, nz):
            g3[group, step] = send(
                owned.at[group],
                zfull.at[group, z_rows(z), :],
                g3_send.at[group, step - 1],
                g3_recv.at[group, step - 1],
                z_peer(step),
            )

    def group_rows(group):
        return pl.ds(GROUPS[group][0] * rows, len(GROUPS[group]) * rows)

    def send_g2(group):
        for step in range(1, nz):
            g3[group, step].wait_recv()
        band = len(GROUPS[group]) * rows
        for colour in range(2):
            slot = (x, y) if colour == 0 else (y, x)
            source = pl.ds(colour * band, band)
            full_ref[core, colour, slot[0], slot[1], group_rows(group), :] = zfull[group, source, :]
            for step in range(1, n):
                g2[group, colour, step] = send(
                    zfull.at[group, source, :],
                    full_ref.at[core, colour, slot[0], slot[1], group_rows(group), :],
                    g2_send.at[group, colour, step - 1],
                    g2_recv.at[group, colour, step - 1],
                    second_peer(colour, step),
                )

    def send_g0(group, colour, position, step):
        piece = full_ref.at[core, colour, position, :, group_rows(group), :]
        g0[group, colour, step] = send(
            piece,
            piece,
            g0_send.at[group, colour, step],
            g0_recv.at[group, colour, step],
            (y, partner),
        )

    def send_g1(group):
        for colour in range(2):
            first = x if colour == 0 else y
            for step in range(1, n):
                g2[group, colour, step].wait_recv()
            piece = full_ref.at[core, colour, first, :, group_rows(group), :]
            for step in range(1, n):
                g1[group, colour, step] = send(
                    piece,
                    piece,
                    g1_send.at[group, colour, step - 1],
                    g1_recv.at[group, colour, step - 1],
                    first_peer(colour, step),
                )
            send_g0(group, colour, first, 0)

    def forward(group):
        for step in range(1, n):
            for colour in range(2):
                g1[group, colour, step].wait_recv()
                first = x if colour == 0 else y
                send_g0(group, colour, (first + n - step) % n, step)

    def load_gfield(lon):
        return gfield[lon]

    def store_sgrad(lon, value):
        sgrad_ref[lon_rows(lon), :] = value

    send_s2(0)
    tail_solve()
    send_s3(0)
    send_s2(1)
    for copy in halo_two:
        copy.wait_recv()
    advance(1, load_gfield, store_sgrad)
    send_s2(2)
    send_s3(1)
    send_g3(0)
    send_s3(2)
    send_g3(1)
    send_g2(0)
    send_g3(2)
    send_g1(0)
    send_g2(1)
    send_g2(2)
    send_g1(1)
    forward(0)
    send_g1(2)
    forward(1)
    forward(2)
    for copy in g0.values():
        copy.wait_recv()
    for copy in sent:
        copy.wait_send()


def unscramble_kernel(
    half, state_ref, sgrad_ref, full_ref, state_out, sgrad_out, mid_out, out_out, in_out, mid, out, inn, sems
):
    _, colours, firsts, seconds, strip, width = full_ref.shape
    rows = strip // CHUNKS
    copies = []

    def emit(src, dst):
        copy = pltpu.make_async_copy(src, dst, sems.at[len(copies)])
        copy.start()
        copies.append(copy)

    emit(state_ref, state_out)
    emit(sgrad_ref, sgrad_out)
    for chunk in range(CHUNKS):
        for colour in range(colours):
            for first in range(firsts):
                row = (colour * firsts + first) * rows
                for slot in range(2 * seconds):
                    block = full_ref[
                        slot // seconds,
                        colour,
                        first,
                        slot % seconds,
                        chunk * rows : (chunk + 1) * rows,
                        :,
                    ].astype(F32)
                    lanes = slice(slot * width, (slot + 1) * width)
                    if chunk < CHUNKS - 1:
                        mid[chunk * CHUNK_ROWS + row : chunk * CHUNK_ROWS + row + rows, lanes] = block
                    elif colour == 0:
                        out[row : row + rows, lanes] = block
                    else:
                        for part in range(width // 128):
                            start = slot * width + part * 128 + first * rows
                            inn[start : start + rows, :] = block[:, part * 128 : (part + 1) * 128]
        if chunk < CHUNKS - 1:
            span = pl.ds(chunk * CHUNK_ROWS, CHUNK_ROWS)
            emit(mid.at[span, :], mid_out.at[span, :])
    emit(out, out_out)
    emit(inn, in_out)
    for copy in copies:
        copy.wait()


def per_device(
    nz, prognostic, diffusivity, mixing, cotangent, tile_cols, pad_mask, tile_count, w_in, w_mid, w_out
):
    n = lax.axis_size("ens")
    fields = prognostic.shape[1]
    levels = diffusivity.shape[1]
    units = w_mid.shape[0]
    half = units // 2
    rows = CHUNK_ROWS // (2 * n)
    width = half // n
    tiles = tile_cols.shape[2]
    groups = len(GROUPS)
    zrows = -(-2 * max(len(g) for g in GROUPS) * rows // (16 * nz)) * 16
    flat = (fields * LONS, 128)
    factor = 1.0 / math.sqrt(n * lax.axis_size("horiz") * LONS * 128)
    dma = pltpu.SemaphoreType.DMA
    vm = pltpu.VMEM
    any_spec = pl.BlockSpec(memory_space=pltpu.HBM)
    vmem_spec = pl.BlockSpec(memory_space=pltpu.VMEM)
    operands = [
        prognostic.reshape(flat),
        diffusivity.reshape(levels * LONS, 128),
        mixing.reshape(2 * LONS, 128),
        cotangent.reshape(flat),
        tile_cols.reshape(tiles, 1, 128),
        pad_mask.reshape(tiles, 1, 128),
        tile_count,
        w_in,
        w_mid,
        w_out,
    ]
    operands = [
        v if v.size == 1 else pltpu.with_memory_space_constraint(v, pltpu.HBM) for v in operands
    ]
    state, sgrad, full = pl.pallas_call(
        functools.partial(window_kernel, (n, nz, levels, fields // levels), factor),
        out_shape=(
            jax.ShapeDtypeStruct(flat, F32),
            jax.ShapeDtypeStruct(flat, F32),
            jax.ShapeDtypeStruct((2, 2, n, n, CHUNKS * rows, width), BF16),
        ),
        in_specs=[any_spec] * 10,
        out_specs=(vmem_spec, vmem_spec, vmem_spec),
        scratch_shapes=[
            vm(flat, F32),
            vm((levels * LONS, 128), F32),
            vm((2 * LONS, 128), F32),
            vm(flat, F32),
            vm((tiles, 1, 128), jnp.int32),
            vm((tiles, 1, 128), jnp.int32),
            pltpu.SMEM((1, 1), jnp.int32),
            vm(w_in.shape, BF16),
            vm(w_mid.shape, BF16),
            vm(w_out.shape, BF16),
            vm((2, 2, 2, fields, 128), BF16),
            vm((2, 2, 2, fields, 128), BF16),
            vm((2, 2 * LONS, 128), F32),
            vm((LONS + 2, fields, 128), F32),
            vm(flat, F32),
            vm((levels * LONS, 128), F32),
            vm((levels * LONS, 128), F32),
            vm(flat, F32),
            vm(flat, F32),
            vm((LONS, fields, 128), F32),
            vm((fields, LONS * 128), BF16),
            vm((fields, LONS * 128), BF16),
            vm((units, LONS * 128), F32),
            vm((units, LONS * 128), F32),
            vm((units, LONS * 128), BF16),
            vm((units, LONS * 128), BF16),
            vm((units, LONS * 128), BF16),
            vm((units, LONS * 128), BF16),
            vm((CHUNKS, 2 * n, rows, half), F32),
            vm((CHUNKS, 2 * n, rows, half), BF16),
            vm((CHUNKS, 2 * n, rows, half), BF16),
            vm((CHUNKS, 2 * n, rows, half), F32),
            vm((CHUNKS, 2 * n, rows, half), BF16),
            vm((2, CHUNKS, n - 1, rows, half), BF16),
            vm((2, CHUNKS, n, rows, width), F32),
            vm((2, CHUNKS, n, rows, width), BF16),
            vm((2, CHUNKS, n - 1, rows, width), BF16),
            vm((groups, zrows * nz, width), F32),
            vm((groups, zrows * nz, width), BF16),
            vm((groups, nz - 1, zrows, width), BF16),
            vm((groups, zrows, width), BF16),
            vm((groups, zrows * nz, width), BF16),
            dma((10,)),
            dma((3, 2)),
            dma((3, 2)),
            dma((CHUNKS,)),
            dma((CHUNKS,)),
            dma((2, CHUNKS, n - 1)),
            dma((2, CHUNKS, n - 1)),
            dma((2, CHUNKS, n - 1)),
            dma((2, CHUNKS, n - 1)),
            dma((groups, nz - 1)),
            dma((groups, nz - 1)),
            dma((groups, nz - 1)),
            dma((groups, nz - 1)),
            dma((groups, 2, n - 1)),
            dma((groups, 2, n - 1)),
            dma((groups, 2, n - 1)),
            dma((groups, 2, n - 1)),
            dma((groups, 2, n)),
            dma((groups, 2, n)),
        ],
        compiler_params=pltpu.CompilerParams(
            collective_id=0, has_side_effects=True, vmem_limit_bytes=40 * 1024 * 1024
        ),
    )(
        *operands
    )
    state, sgrad, grad_mid, grad_out, grad_in = pl.pallas_call(
        functools.partial(unscramble_kernel, half),
        out_shape=(
            jax.ShapeDtypeStruct(flat, F32),
            jax.ShapeDtypeStruct(flat, F32),
            jax.ShapeDtypeStruct(w_mid.shape, F32),
            jax.ShapeDtypeStruct(w_out.shape, F32),
            jax.ShapeDtypeStruct(w_in.shape, F32),
        ),
        in_specs=[vmem_spec] * 3,
        out_specs=(pl.BlockSpec(memory_space=pltpu.HBM),) * 5,
        scratch_shapes=[
            vm(w_mid.shape, F32),
            vm(w_out.shape, F32),
            vm(w_in.shape, F32),
            dma((CHUNKS + 3,)),
        ],
        compiler_params=pltpu.CompilerParams(vmem_limit_bytes=16 * 1024 * 1024),
    )(state, sgrad, full)
    return (
        state.reshape(prognostic.shape),
        sgrad.reshape(prognostic.shape),
        grad_in,
        grad_mid,
        grad_out,
    )


def solution(mesh):
    placed = (
        P("ens", None, "horiz", None),
        P("ens", None, "horiz", None),
        P(None, "horiz", None),
        P("ens", None, "horiz", None),
        P("ens", "horiz", None, None),
        P("ens", "horiz", None, None),
        P("ens", "horiz"),
        P(),
        P(),
        P(),
    )
    nz = mesh.shape["horiz"] // (2 * mesh.shape["ens"])
    return jax.shard_map(
        functools.partial(per_device, nz),
        mesh=mesh,
        in_specs=placed,
        out_specs=(P("ens", None, "horiz", None), P("ens", None, "horiz", None), P(), P(), P()),
        check_vma=False,
    )
```

```python
import functools
import math

import jax
import jax.numpy as jnp
from jax import lax
from jax.experimental import pallas as pl
from jax.experimental.pallas import tpu as pltpu
from jax.sharding import PartitionSpec as P

MESH = pl.DeviceIdType.MESH
LONS = 4
CHUNKS = 5
GROUPS = ((0, 1), (2, 3), (4,))
CHUNK_ROWS = 256
F32 = jnp.float32
BF16 = jnp.bfloat16
NT = (((1,), (1,)), ((), ()))
TN = (((0,), (0,)), ((), ()))


def sigmoid(value):
    return 0.5 * jnp.tanh(0.5 * value) + 0.5


def window_kernel(
    sizes,
    factor,
    prog_hbm,
    diff_hbm,
    mix_hbm,
    cot_hbm,
    cols_hbm,
    pad_hbm,
    count_hbm,
    win_hbm,
    wmid_hbm,
    wout_hbm,
    state_ref,
    sgrad_ref,
    full_ref,
    prog,
    diff,
    mix,
    cot,
    cols,
    pad,
    count,
    w_in,
    w_mid,
    w_out,
    halo_out,
    halo_in,
    mix_in,
    mid_step,
    moved,
    recip,
    ratio,
    adj,
    forced,
    gfield,
    x_half,
    adj_half,
    back_two,
    slope_one,
    act_one,
    act_two,
    delta_one,
    delta_two,
    part_f,
    part_b,
    got0,
    sum1_f,
    sum1_b,
    got1,
    sum2_f,
    sum2_b,
    got2,
    sum3_f,
    sum3_b,
    got3,
    owned,
    zfull,
    load_sem,
    halo_send,
    halo_recv,
    s0_send,
    s0_recv,
    s1_send,
    s1_recv,
    s2_send,
    s2_recv,
    s3_send,
    s3_recv,
    g3_send,
    g3_recv,
    g2_send,
    g2_recv,
    g1_send,
    g1_recv,
    g0_send,
    g0_recv,
):
    n, nz, levels, variables = sizes
    fields = levels * variables
    units = w_mid.shape[0]
    half = units // 2
    ring = n * nz * 2
    y = lax.axis_index("ens")
    h = lax.axis_index("horiz")
    core = h % 2
    z = (h // 2) % nz
    x = h // (2 * nz)
    right = (h + 1) % ring
    left = (h + ring - 1) % ring
    partner = h + 1 - 2 * core
    pieces = 2 * n
    rows = CHUNK_ROWS // pieces
    width = half // n
    zrows = owned.shape[1]

    def at_x(step):
        return (x + step) % n

    def at_y(step):
        return (y + step) % n

    def at_z(step):
        return (z + step) % nz

    def place(xi, zi, ci):
        return (xi * nz + zi) * 2 + ci

    barrier = pltpu.get_barrier_semaphore()
    greeted = [(at_y(s), h) for s in range(1, n)]
    greeted += [(y, place(at_x(s), z, core)) for s in range(1, n)]
    greeted += [(y, place(x, at_z(s), core)) for s in range(1, nz)]
    greeted += [(y, right), (y, left)]
    for peer in greeted:
        pl.semaphore_signal(barrier, inc=1, device_id=peer, device_id_type=MESH)

    loads = []
    for slot, (source, target) in enumerate(
        [
            (prog_hbm, prog),
            (mix_hbm, mix),
            (cols_hbm, cols),
            (pad_hbm, pad),
            (count_hbm, count),
            (diff_hbm, diff),
            (cot_hbm, cot),
            (wout_hbm, w_out),
            (win_hbm, w_in),
            (wmid_hbm, w_mid),
        ]
    ):
        copy = pltpu.make_async_copy(source, target, load_sem.at[slot])
        copy.start()
        loads.append(copy)

    sent = []

    def send(src, dst, send_sem, recv_sem, peer):
        copy = pltpu.make_async_remote_copy(
            src_ref=src,
            dst_ref=dst,
            send_sem=send_sem,
            recv_sem=recv_sem,
            device_id=peer,
            device_id_type=MESH,
        )
        copy.start()
        sent.append(copy)
        return copy

    def lon_rows(lon):
        return pl.ds(lon, fields, stride=LONS)

    def lon_cols(lon):
        return pl.ds(lon * 128, 128)

    def send_halo(which):
        return [
            send(
                halo_out.at[which, 0],
                halo_in.at[which, 0],
                halo_send.at[which, 0],
                halo_recv.at[which, 0],
                (y, right),
            ),
            send(
                halo_out.at[which, 1],
                halo_in.at[which, 1],
                halo_send.at[which, 1],
                halo_recv.at[which, 1],
                (y, left),
            ),
        ]

    loads[0].wait()
    for lon in range(LONS):
        halo_out[0, 1 - lon // 2, lon % 2] = prog[lon_rows(lon), :].astype(BF16)
    loads[1].wait()
    pl.semaphore_wait(barrier, len(greeted))
    halo_one = send_halo(0)
    mix_copies = [
        send(mix, mix_in.at[0], halo_send.at[2, 0], halo_recv.at[2, 0], (y, right)),
        send(mix, mix_in.at[1], halo_send.at[2, 1], halo_recv.at[2, 1], (y, left)),
    ]

    for copy in loads[2:7]:
        copy.wait()
    lon_of = lax.broadcasted_iota(jnp.int32, (16, 128), 0)
    lat_of = lax.broadcasted_iota(jnp.int32, (128, 128), 0)
    used = count[0, 0]
    live = jnp.zeros((16, 128), F32)
    for tile in range(cols.shape[0]):
        column = cols[tile]
        flag = jnp.where(tile < used, pad[tile], 0)
        lon_hit = (lon_of == column // 128) & (jnp.broadcast_to(flag, (16, 128)) > 0)
        lat_hit = lat_of == column % 128
        live = live + lax.dot_general(
            jnp.where(lon_hit, 1.0, 0.0).astype(BF16),
            jnp.where(lat_hit, 1.0, 0.0).astype(BF16),
            NT,
            preferred_element_type=F32,
        )
    live4 = live[:LONS]

    def level_rows(var, level):
        return pl.ds((var * levels + level) * LONS, LONS)

    def coefficient(level):
        return diff[level * LONS : (level + 1) * LONS, :].astype(BF16).astype(F32)

    below = jnp.zeros((LONS, 128), F32)
    last_ratio = jnp.zeros((LONS, 128), F32)
    swept = [jnp.zeros((LONS, 128), F32) for _ in range(variables)]
    for level in range(levels):
        here = coefficient(level)
        inverse = 1.0 / (1.0 + below + here + below * last_ratio)
        last_ratio = -here * inverse
        recip[level * LONS : (level + 1) * LONS, :] = inverse
        ratio[level * LONS : (level + 1) * LONS, :] = last_ratio
        for var in range(variables):
            right_side = (cot[level_rows(var, level), :] * live4).astype(BF16).astype(F32)
            swept[var] = (right_side + below * swept[var]) * inverse
            adj[level_rows(var, level), :] = swept[var]
        below = here

    def sweep_down(load_right, work):
        value = [jnp.zeros((LONS, 128), F32) for _ in range(variables)]
        lower = jnp.zeros((LONS, 128), F32)
        for level in range(levels):
            inverse = recip[level * LONS : (level + 1) * LONS, :]
            for var in range(variables):
                value[var] = (load_right(var, level) + lower * value[var]) * inverse
                work[level_rows(var, level), :] = value[var]
            lower = coefficient(level)

    def sweep_up(work, store):
        value = [work[level_rows(var, levels - 1), :] for var in range(variables)]
        for var in range(variables):
            store(var, levels - 1, value[var])
        for level in range(levels - 2, -1, -1):
            back = ratio[level * LONS : (level + 1) * LONS, :]
            for var in range(variables):
                value[var] = work[level_rows(var, level), :] - back * value[var]
                store(var, level, value[var])

    def store_adj(var, level, value):
        adj[level_rows(var, level), :] = value

    sweep_up(adj, store_adj)
    for lon in range(LONS):
        adj_half[:, lon_cols(lon)] = adj[lon_rows(lon), :].astype(BF16)
    loads[7].wait()
    back_two[...] = lax.dot_general(w_out[...], adj_half[...], TN, preferred_element_type=F32)

    for copy in mix_copies:
        copy.wait_recv()
    lane = lax.broadcasted_iota(jnp.int32, (2 * LONS, 128), 1)
    mixes = [mix_in[0], mix[...], mix_in[1]]
    norths = [jnp.where(lane == 127, 0.0, m) for m in mixes]
    souths = [jnp.where(lane == 0, 0.0, pltpu.roll(m, 1, 1)) for m in mixes]

    def mix_row(tables, lon, offset):
        row = lon % LONS + offset
        return tables[lon // LONS + 1][row : row + 1]

    weights = []
    for lon in range(-1, LONS + 1):
        east = mix_row(mixes, lon, 0)
        west = mix_row(mixes, lon - 1, 0)
        north = mix_row(norths, lon, LONS)
        south = mix_row(souths, lon, LONS)
        weights.append((1.0 - east - west - north - south, east, west, north, south))

    def stencil(lon, west_val, own, east_val):
        centre, east, west, north, south = weights[lon + 1]
        return (
            centre * own
            + east * east_val
            + west * west_val
            + north * pltpu.roll(own, 127, 1)
            + south * pltpu.roll(own, 1, 1)
        )

    def advance(which, load_own, store):
        def load(lon):
            if lon < 0:
                return halo_in[which, 0, lon + 2].astype(F32)
            if lon >= LONS:
                return halo_in[which, 1, lon - LONS].astype(F32)
            return load_own(lon)

        for lon in range(-1, LONS + 1):
            mid_step[lon + 1] = stencil(lon, load(lon - 1), load(lon), load(lon + 1))
        for lon in range(LONS):
            store(lon, stencil(lon, mid_step[lon], mid_step[lon + 1], mid_step[lon + 2]))

    def load_prog(lon):
        return prog[lon_rows(lon), :]

    def store_moved(lon, value):
        moved[lon_rows(lon), :] = value
        x_half[:, lon_cols(lon)] = value.astype(BF16)

    for copy in halo_one:
        copy.wait_recv()
    advance(0, load_prog, store_moved)

    loads[8].wait()
    for block in range(units // CHUNK_ROWS):
        span = slice(block * CHUNK_ROWS, (block + 1) * CHUNK_ROWS)
        pre = jnp.dot(w_in[span, :], x_half[...], preferred_element_type=F32)
        sig = sigmoid(pre)
        act_one[span, :] = (pre * sig).astype(BF16)
        slope_one[span, :] = sig * (1.0 + pre * (1.0 - sig))

    other = 1 - core

    def side_rows(side):
        return pl.ds(pl.multiple_of(side * half, half), half)

    def chunk_half(chunk, side):
        if chunk < CHUNKS - 1:
            left_side = delta_two[chunk * CHUNK_ROWS : (chunk + 1) * CHUNK_ROWS, :]
            value = lax.dot_general(
                left_side, act_one[side_rows(side), :], NT, preferred_element_type=F32
            )
        else:
            top = lax.dot_general(
                adj_half[...], act_two[side_rows(side), :], NT, preferred_element_type=F32
            )
            low = lax.dot_general(
                delta_one[side_rows(side), :], x_half[...], NT, preferred_element_type=F32
            )
            low = jnp.concatenate(
                [low[b * 128 : (b + 1) * 128, :] for b in range(half // 128)], axis=1
            )
            value = jnp.concatenate([top, low], axis=0)
        return value.reshape(pieces, rows, half)

    s0 = []

    def send_s0(chunk):
        part_b[chunk] = chunk_half(chunk, other).astype(BF16)
        s0.append(
            send(
                part_b.at[chunk],
                got0.at[chunk],
                s0_send.at[chunk],
                s0_recv.at[chunk],
                (y, partner),
            )
        )

    s1 = []

    def send_s1(chunk):
        s0[chunk].wait_recv()
        total = part_f[chunk] + got0[chunk].astype(F32)
        sum1_f[chunk] = total
        sum1_b[chunk] = total.astype(BF16)
        copies = ([], [])
        for step in range(1, n):
            copies[0].append(
                send(
                    sum1_b.at[chunk, at_x(step)],
                    got1.at[0, chunk, step - 1],
                    s1_send.at[0, chunk, step - 1],
                    s1_recv.at[0, chunk, step - 1],
                    (y, place(at_x(step), z, core)),
                )
            )
            copies[1].append(
                send(
                    sum1_b.at[chunk, n + at_y(step)],
                    got1.at[1, chunk, step - 1],
                    s1_send.at[1, chunk, step - 1],
                    s1_recv.at[1, chunk, step - 1],
                    (at_y(step), h),
                )
            )
        s1.append(copies)

    loads[9].wait()
    for block in range(units // CHUNK_ROWS):
        span = slice(block * CHUNK_ROWS, (block + 1) * CHUNK_ROWS)
        pre = jnp.dot(w_mid[span, :], act_one[...], preferred_element_type=F32)
        sig = sigmoid(pre)
        act_two[span, :] = (pre * sig).astype(BF16)
        delta = (back_two[span, :] * (sig * (1.0 + pre * (1.0 - sig)))).astype(BF16)
        delta_two[span, :] = delta

    def keep_half(chunk):
        part_f[chunk] = chunk_half(chunk, core)

    for chunk in range(CHUNKS - 1):
        send_s0(chunk)
    for chunk in range(CHUNKS - 1):
        keep_half(chunk)
        send_s1(chunk)
    for block in range(units // CHUNK_ROWS):
        span = slice(block * CHUNK_ROWS, (block + 1) * CHUNK_ROWS)
        back = lax.dot_general(w_mid[:, span], delta_two[...], TN, preferred_element_type=F32)
        delta_one[span, :] = (back * slope_one[span, :]).astype(BF16)
    send_s0(CHUNKS - 1)
    keep_half(CHUNKS - 1)
    back_x = lax.dot_general(w_in[...], delta_one[...], TN, preferred_element_type=F32)
    for lon in range(LONS):
        fresh = adj[lon_rows(lon), :] + back_x[:, lon * 128 : (lon + 1) * 128]
        value = jnp.where(
            jnp.broadcast_to(live[lon : lon + 1], (fields, 128)) > 0.5,
            fresh.astype(BF16).astype(F32),
            cot[lon_rows(lon), :],
        )
        gfield[lon] = value
        halo_out[1, 1 - lon // 2, lon % 2] = value.astype(BF16)
    halo_two = send_halo(1)
    send_s1(CHUNKS - 1)

    def load_forced(var, level):
        return forced[level_rows(var, level), :]

    def store_state(var, level, value):
        here = level_rows(var, level)
        state_ref[here, :] = jnp.where(
            live4 > 0.5, value.astype(BF16).astype(F32), moved[here, :]
        )

    def tail_down():
        tendency = jnp.dot(w_out[...], act_two[...], preferred_element_type=F32)
        for lon in range(LONS):
            forced[lon_rows(lon), :] = (
                x_half[:, lon_cols(lon)].astype(F32) + tendency[:, lon * 128 : (lon + 1) * 128]
            )

        sweep_down(load_forced, forced)

    def tail_up():
        sweep_up(forced, store_state)

    own1 = (x, n + y)
    own2 = (y, x)
    s2, s3, g3, g2, g1, g0 = {}, {}, {}, {}, {}, {}

    def first_peer(colour, step):
        return (y, place(at_x(step), z, core)) if colour == 0 else (at_y(step), h)

    def second_peer(colour, step):
        return (at_y(step), h) if colour == 0 else (y, place(at_x(step), z, core))

    def send_s2(group):
        for chunk in GROUPS[group]:
            for colour in range(2):
                total = sum1_f[chunk, own1[colour]]
                for step in range(n - 1):
                    s1[chunk][colour][step].wait_recv()
                    total = total + got1[colour, chunk, step].astype(F32)
                for slot in range(n):
                    block = total[:, slot * width : (slot + 1) * width]
                    sum2_f[colour, chunk, slot] = block
                    sum2_b[colour, chunk, slot] = block.astype(BF16)
                for step in range(1, n):
                    s2[chunk, colour, step] = send(
                        sum2_b.at[colour, chunk, at_y(step) if colour == 0 else at_x(step)],
                        got2.at[colour, chunk, step - 1],
                        s2_send.at[colour, chunk, step - 1],
                        s2_recv.at[colour, chunk, step - 1],
                        second_peer(colour, step),
                    )

    def z_rows(zi):
        return pl.ds(pl.multiple_of(zi * zrows, 8), zrows)

    def z_peer(step):
        return (y, place(x, at_z(step), core))

    def send_s3(group):
        chunks = GROUPS[group]
        filled = 2 * len(chunks) * rows
        if zrows * nz > filled:
            sum3_f[group, filled:, :] = jnp.zeros((zrows * nz - filled, width), F32)
            sum3_b[group, filled:, :] = jnp.zeros((zrows * nz - filled, width), BF16)
        for colour in range(2):
            for slot, chunk in enumerate(chunks):
                total = sum2_f[colour, chunk, own2[colour]]
                for step in range(1, n):
                    s2[chunk, colour, step].wait_recv()
                    total = total + got2[colour, chunk, step - 1].astype(F32)
                start = (colour * len(chunks) + slot) * rows
                sum3_f[group, start : start + rows, :] = total
                sum3_b[group, start : start + rows, :] = total.astype(BF16)
        for step in range(1, nz):
            s3[group, step] = send(
                sum3_b.at[group, z_rows(at_z(step)), :],
                got3.at[group, step - 1],
                s3_send.at[group, step - 1],
                s3_recv.at[group, step - 1],
                z_peer(step),
            )

    def send_g3(group):
        total = sum3_f[group, z_rows(z), :]
        for step in range(1, nz):
            s3[group, step].wait_recv()
            total = total + got3[group, step - 1].astype(F32)
        mine = (total * factor).astype(BF16)
        owned[group] = mine
        zfull[group, z_rows(z), :] = mine
        for step in range(1, nz):
            g3[group, step] = send(
                owned.at[group],
                zfull.at[group, z_rows(z), :],
                g3_send.at[group, step - 1],
                g3_recv.at[group, step - 1],
                z_peer(step),
            )

    def group_rows(group):
        return pl.ds(GROUPS[group][0] * rows, len(GROUPS[group]) * rows)

    def send_g2(group):
        for step in range(1, nz):
            g3[group, step].wait_recv()
        band = len(GROUPS[group]) * rows
        for colour in range(2):
            slot = (x, y) if colour == 0 else (y, x)
            source = pl.ds(colour * band, band)
            full_ref[core, colour, slot[0], slot[1], group_rows(group), :] = zfull[group, source, :]
            for step in range(1, n):
                g2[group, colour, step] = send(
                    zfull.at[group, source, :],
                    full_ref.at[core, colour, slot[0], slot[1], group_rows(group), :],
                    g2_send.at[group, colour, step - 1],
                    g2_recv.at[group, colour, step - 1],
                    second_peer(colour, step),
                )

    def send_g0(group, colour, position, step):
        piece = full_ref.at[core, colour, position, :, group_rows(group), :]
        g0[group, colour, step] = send(
            piece,
            piece,
            g0_send.at[group, colour, step],
            g0_recv.at[group, colour, step],
            (y, partner),
        )

    def send_g1(group):
        for colour in range(2):
            first = x if colour == 0 else y
            for step in range(1, n):
                g2[group, colour, step].wait_recv()
            piece = full_ref.at[core, colour, first, :, group_rows(group), :]
            for step in range(1, n):
                g1[group, colour, step] = send(
                    piece,
                    piece,
                    g1_send.at[group, colour, step - 1],
                    g1_recv.at[group, colour, step - 1],
                    first_peer(colour, step),
                )
            send_g0(group, colour, first, 0)

    def forward(group):
        for step in range(1, n):
            for colour in range(2):
                g1[group, colour, step].wait_recv()
                first = x if colour == 0 else y
                send_g0(group, colour, (first + n - step) % n, step)

    def load_gfield(lon):
        return gfield[lon]

    def store_sgrad(lon, value):
        sgrad_ref[lon_rows(lon), :] = value

    send_s2(0)
    tail_down()
    tail_up()
    send_s2(1)
    for copy in halo_two:
        copy.wait_recv()
    advance(1, load_gfield, store_sgrad)
    send_s2(2)
    for stage in (send_s3, send_g3, send_g2, send_g1, forward):
        for group in range(len(GROUPS)):
            stage(group)
    for copy in g0.values():
        copy.wait_recv()
    for copy in sent:
        copy.wait_send()


def unscramble_kernel(
    half, state_ref, sgrad_ref, full_ref, state_out, sgrad_out, mid_out, out_out, in_out, mid, out, inn, sems
):
    _, colours, firsts, seconds, strip, width = full_ref.shape
    rows = strip // CHUNKS
    copies = []

    def emit(src, dst):
        copy = pltpu.make_async_copy(src, dst, sems.at[len(copies)])
        copy.start()
        copies.append(copy)

    emit(state_ref, state_out)
    emit(sgrad_ref, sgrad_out)
    for chunk in range(CHUNKS):
        for colour in range(colours):
            for first in range(firsts):
                row = (colour * firsts + first) * rows
                for slot in range(2 * seconds):
                    block = full_ref[
                        slot // seconds,
                        colour,
                        first,
                        slot % seconds,
                        chunk * rows : (chunk + 1) * rows,
                        :,
                    ].astype(F32)
                    lanes = slice(slot * width, (slot + 1) * width)
                    if chunk < CHUNKS - 1:
                        mid[chunk * CHUNK_ROWS + row : chunk * CHUNK_ROWS + row + rows, lanes] = block
                    elif colour == 0:
                        out[row : row + rows, lanes] = block
                    else:
                        for part in range(width // 128):
                            start = slot * width + part * 128 + first * rows
                            inn[start : start + rows, :] = block[:, part * 128 : (part + 1) * 128]
        if chunk < CHUNKS - 1:
            span = pl.ds(chunk * CHUNK_ROWS, CHUNK_ROWS)
            emit(mid.at[span, :], mid_out.at[span, :])
    emit(out, out_out)
    emit(inn, in_out)
    for copy in copies:
        copy.wait()


def per_device(
    nz, prognostic, diffusivity, mixing, cotangent, tile_cols, pad_mask, tile_count, w_in, w_mid, w_out
):
    n = lax.axis_size("ens")
    fields = prognostic.shape[1]
    levels = diffusivity.shape[1]
    units = w_mid.shape[0]
    half = units // 2
    rows = CHUNK_ROWS // (2 * n)
    width = half // n
    tiles = tile_cols.shape[2]
    groups = len(GROUPS)
    zrows = -(-2 * max(len(g) for g in GROUPS) * rows // (8 * nz)) * 8
    flat = (fields * LONS, 128)
    factor = 1.0 / math.sqrt(n * lax.axis_size("horiz") * LONS * 128)
    dma = pltpu.SemaphoreType.DMA
    vm = pltpu.VMEM
    any_spec = pl.BlockSpec(memory_space=pltpu.HBM)
    vmem_spec = pl.BlockSpec(memory_space=pltpu.VMEM)
    operands = [
        prognostic.reshape(flat),
        diffusivity.reshape(levels * LONS, 128),
        mixing.reshape(2 * LONS, 128),
        cotangent.reshape(flat),
        tile_cols.reshape(tiles, 1, 128),
        pad_mask.reshape(tiles, 1, 128),
        tile_count,
        w_in,
        w_mid,
        w_out,
    ]
    operands = [
        v if v.size == 1 else pltpu.with_memory_space_constraint(v, pltpu.HBM) for v in operands
    ]
    state, sgrad, full = pl.pallas_call(
        functools.partial(window_kernel, (n, nz, levels, fields // levels), factor),
        out_shape=(
            jax.ShapeDtypeStruct(flat, F32),
            jax.ShapeDtypeStruct(flat, F32),
            jax.ShapeDtypeStruct((2, 2, n, n, CHUNKS * rows, width), BF16),
        ),
        in_specs=[any_spec] * 10,
        out_specs=(vmem_spec, vmem_spec, vmem_spec),
        scratch_shapes=[
            vm(flat, F32),
            vm((levels * LONS, 128), F32),
            vm((2 * LONS, 128), F32),
            vm(flat, F32),
            vm((tiles, 1, 128), jnp.int32),
            vm((tiles, 1, 128), jnp.int32),
            pltpu.SMEM((1, 1), jnp.int32),
            vm(w_in.shape, BF16),
            vm(w_mid.shape, BF16),
            vm(w_out.shape, BF16),
            vm((2, 2, 2, fields, 128), BF16),
            vm((2, 2, 2, fields, 128), BF16),
            vm((2, 2 * LONS, 128), F32),
            vm((LONS + 2, fields, 128), F32),
            vm(flat, F32),
            vm((levels * LONS, 128), F32),
            vm((levels * LONS, 128), F32),
            vm(flat, F32),
            vm(flat, F32),
            vm((LONS, fields, 128), F32),
            vm((fields, LONS * 128), BF16),
            vm((fields, LONS * 128), BF16),
            vm((units, LONS * 128), F32),
            vm((units, LONS * 128), F32),
            vm((units, LONS * 128), BF16),
            vm((units, LONS * 128), BF16),
            vm((units, LONS * 128), BF16),
            vm((units, LONS * 128), BF16),
            vm((CHUNKS, 2 * n, rows, half), F32),
            vm((CHUNKS, 2 * n, rows, half), BF16),
            vm((CHUNKS, 2 * n, rows, half), BF16),
            vm((CHUNKS, 2 * n, rows, half), F32),
            vm((CHUNKS, 2 * n, rows, half), BF16),
            vm((2, CHUNKS, n - 1, rows, half), BF16),
            vm((2, CHUNKS, n, rows, width), F32),
            vm((2, CHUNKS, n, rows, width), BF16),
            vm((2, CHUNKS, n - 1, rows, width), BF16),
            vm((groups, zrows * nz, width), F32),
            vm((groups, zrows * nz, width), BF16),
            vm((groups, nz - 1, zrows, width), BF16),
            vm((groups, zrows, width), BF16),
            vm((groups, zrows * nz, width), BF16),
            dma((10,)),
            dma((3, 2)),
            dma((3, 2)),
            dma((CHUNKS,)),
            dma((CHUNKS,)),
            dma((2, CHUNKS, n - 1)),
            dma((2, CHUNKS, n - 1)),
            dma((2, CHUNKS, n - 1)),
            dma((2, CHUNKS, n - 1)),
            dma((groups, nz - 1)),
            dma((groups, nz - 1)),
            dma((groups, nz - 1)),
            dma((groups, nz - 1)),
            dma((groups, 2, n - 1)),
            dma((groups, 2, n - 1)),
            dma((groups, 2, n - 1)),
            dma((groups, 2, n - 1)),
            dma((groups, 2, n)),
            dma((groups, 2, n)),
        ],
        compiler_params=pltpu.CompilerParams(
            collective_id=0, has_side_effects=True, vmem_limit_bytes=40 * 1024 * 1024
        ),
    )(
        *operands
    )
    state, sgrad, grad_mid, grad_out, grad_in = pl.pallas_call(
        functools.partial(unscramble_kernel, half),
        out_shape=(
            jax.ShapeDtypeStruct(flat, F32),
            jax.ShapeDtypeStruct(flat, F32),
            jax.ShapeDtypeStruct(w_mid.shape, F32),
            jax.ShapeDtypeStruct(w_out.shape, F32),
            jax.ShapeDtypeStruct(w_in.shape, F32),
        ),
        in_specs=[vmem_spec] * 3,
        out_specs=(pl.BlockSpec(memory_space=pltpu.HBM),) * 5,
        scratch_shapes=[
            vm(w_mid.shape, F32),
            vm(w_out.shape, F32),
            vm(w_in.shape, F32),
            dma((CHUNKS + 3,)),
        ],
        compiler_params=pltpu.CompilerParams(vmem_limit_bytes=16 * 1024 * 1024),
    )(state, sgrad, full)
    return (
        state.reshape(prognostic.shape),
        sgrad.reshape(prognostic.shape),
        grad_in,
        grad_mid,
        grad_out,
    )


def solution(mesh):
    placed = (
        P("ens", None, "horiz", None),
        P("ens", None, "horiz", None),
        P(None, "horiz", None),
        P("ens", None, "horiz", None),
        P("ens", "horiz", None, None),
        P("ens", "horiz", None, None),
        P("ens", "horiz"),
        P(),
        P(),
        P(),
    )
    nz = mesh.shape["horiz"] // (2 * mesh.shape["ens"])
    return jax.shard_map(
        functools.partial(per_device, nz),
        mesh=mesh,
        in_specs=placed,
        out_specs=(P("ens", None, "horiz", None), P("ens", None, "horiz", None), P(), P(), P()),
        check_vma=False,
    )
```
